256 devices in a mesh: shot: 32 (over y, x, core), freq: 8 (over z).
Axes of the slice: x: 4, y: 4, z: 8, core: 2. Of those that a mesh axis runs over, the one named last changes fastest.
Arguments:
- traces: float32 [128, 2048, 1024], P('shot', 'freq'), may hold values from -6 to 6
- interp_weights: float32 [128, 16, 128, 128], P('shot'), may hold values from -0.09375 to 0.09375
- tile_ids: int32 [128, 16], P('shot'), may hold values from 0 to 63, as said below
Outputs:
- binned: float32 [64, 2, 384, 128], P('shot', None, 'freq')
The draws below stay inside these ranges and needn't reach their ends.
Inputs may be any that keep to these rules, and one draw needn't show every extreme that they name: `tile_ids`: tile g is owned by index g // 2 of shot. Among the receiver blocks of the shots of one index of shot, at most 4 land on tiles of one owner, and in every draw each index of shot sends exactly 4 to one owner.
All inputs are finite; a program needn't handle non-finite values.
Results may differ from the reference program's by a relative error of at most 0.0003.
Values sent between devices are 32-bit elements; how exact they have to be, the bound alone decides.
A program may use at most 64 MiB of HBM per device.

```python
import math
import jax
import jax.numpy as jnp
from jax import lax

SH_DEV = 4
RECS = 2048
NT = 1024
NF = 384
RB = 128
TILE = 128
TILES_DEV = 2
SHOTS = 128
NRB = 16
NTILES = 64
CAP = 4


def draw_tile_ids(key, part):
    owners = NTILES // TILES_DEV
    row_count = SH_DEV * NRB
    block_count = SHOTS // SH_DEV

    def one_block(block_key):
        key_hot, key_shift, key_perm, key_sub = jax.random.split(block_key, 4)
        hottest = jax.random.randint(key_hot, (), 0, owners)
        offset = jax.random.randint(key_shift, (), 0, owners - 1)
        position = jnp.arange(row_count, dtype=jnp.int32)
        others = (hottest + 1 + (position - CAP + offset) % (owners - 1)) % owners
        target = jnp.where(position < CAP, hottest, others)
        order = jax.random.permutation(key_perm, row_count)
        target = target[order]
        within = jax.random.randint(key_sub, (row_count,), 0, TILES_DEV)
        return (target * TILES_DEV + within).astype(jnp.int32)
    block_keys = jax.random.split(jax.random.fold_in(key, 7), block_count)
    return jax.vmap(one_block)(block_keys).reshape(SHOTS, NRB)


def level_of(key, dims, shards, smallest, top_value):
    level = 1.0
    for dim, blocks in shards:
        steps = jax.random.uniform(jax.random.fold_in(jax.random.fold_in(key, 6), dim), (blocks,), jnp.float32, smallest / len(shards), top_value / len(shards))
        level = level * jnp.repeat(jnp.exp(steps), dims[dim] // blocks).reshape((-1,) + (1,) * (len(dims) - 1 - dim))
    return level


def bell_draw(key, dims, width, bound, cuts=(), kind=jnp.bfloat16):
    level = level_of(key, dims, cuts, -0.22, 0.18) if cuts else 1.0
    result = jax.random.normal(key, dims, jnp.float32) * width * level
    return jnp.minimum(jnp.maximum(result, -bound), bound).astype(kind)


def setup_inputs(seed: int = 0) -> dict:
    arg_keys = jax.random.split(jax.random.key(seed), 4)
    traces = bell_draw(arg_keys[0], (SHOTS, RECS, NT), 1.0, 6.0, ((0, 32), (1, 8)), jnp.float32)
    interp_weights = bell_draw(arg_keys[1], (SHOTS, NRB, RB, TILE), (RB * SH_DEV * NRB // TILES_DEV) ** -0.5, 0.09375, ((0, 32),), jnp.float32)
    tile_ids = draw_tile_ids(jax.random.fold_in(arg_keys[3], 71), 0)
    return dict(traces=traces, interp_weights=interp_weights, tile_ids=tile_ids)


def reference(traces, interp_weights, tile_ids):

    def one_shot(binned, shot_data):
        gather_t, weights, tile_row = shot_data
        spec = jnp.fft.rfft(gather_t, axis=-1)[:, :NF] / math.sqrt(NT)
        parts = jnp.stack([jnp.real(spec), jnp.imag(spec)])
        parts = jnp.transpose(parts, (0, 2, 1)).reshape(2 * NF, NRB, RB)
        partial_value = jnp.einsum('cbr,brt->bct', parts, weights, precision=lax.Precision.HIGHEST)
        onehot = (tile_row[None, :] == jnp.arange(NTILES, dtype=jnp.int32)[:, None]).astype(partial_value.dtype)
        added = jnp.dot(onehot, partial_value.reshape(NRB, 2 * NF * TILE), precision=lax.Precision.HIGHEST)
        return (binned + added, None)
    start = jnp.zeros((NTILES, 2 * NF * TILE), jnp.float32)
    binned, unused = lax.scan(one_shot, start, (traces, interp_weights, tile_ids))
    return binned.reshape(NTILES, 2, NF, TILE)
```

```python
import math

import jax
import jax.numpy as jnp
import numpy as np
from jax import lax
from jax.experimental import pallas as pl
from jax.experimental.pallas import tpu as pltpu
from jax.sharding import PartitionSpec as P

NF = 384
TILES_DEV = 2
YS, XS, CS = 4, 4, 2
PLANE = YS * XS * CS
ZS = 8
ROWS = 8
MESH = pl.DeviceIdType.MESH


def tables(time_len, per):
    t = np.arange(time_len)
    low = 2.0 * math.pi / time_len * (np.arange(per)[:, None] * t[None, :] % time_len)
    base = np.concatenate([np.cos(low), np.sin(low)]) / math.sqrt(time_len)
    high = 2.0 * math.pi / time_len * ((np.arange(ZS) * per)[:, None] * t[None, :] % time_len)
    turn = np.stack([np.cos(high), np.sin(high)], axis=1)
    return base.astype(np.float32), turn.astype(np.float32)


def split(value):
    high = value.astype(jnp.bfloat16)
    return high, (value - high.astype(jnp.float32)).astype(jnp.bfloat16)


def nt_dot(a, b):
    return lax.dot_general(a, b, (((1,), (1,)), ((), ())), preferred_element_type=jnp.float32)


def nn_dot(a, b):
    return jnp.dot(a, b, preferred_element_type=jnp.float32)


def kernel(
    ids_ref, base_ref, turn_ref, traces_ref, weights_ref, out_ref,
    tr, tr_hi, tr_lo, wt, wt_hi, wt_lo, table, send, recv, zsend, zrecv,
    id_send, id_recv, onehot, fsend, frecv,
    load_sem, wload_sem, send_sem, recv_sem, self_sem, zsend_sem, zrecv_sem,
    id_send_sem, id_recv_sem, fsend_sem, frecv_sem, fself_sem,
):
    per = base_ref.shape[0] // 2
    both = 2 * per
    share = both // PLANE
    tiles = PLANE * TILES_DEV
    me = lax.axis_index("shot")
    z = lax.axis_index("freq")
    core = me % CS
    x = me // CS % XS
    y = me // (CS * XS)

    def peer(r):
        py = (y + r // (CS * XS)) % YS
        px = (x + r // CS % XS) % XS
        pc = (core + r) % CS
        return (py * XS + px) * CS + pc

    barrier = pltpu.get_barrier_semaphore()

    def greet(r, carry):
        pl.semaphore_signal(barrier, inc=1, device_id=(peer(r), z), device_id_type=MESH)
        return carry

    lax.fori_loop(1, PLANE, greet, 0)
    for step in (1, ZS - 1):
        pl.semaphore_signal(
            barrier, inc=1, device_id=(me, (z + step) % ZS), device_id_type=MESH
        )

    shots = traces_ref.shape[0]
    per_shot = traces_ref.shape[1]
    loads = []
    for s in range(shots):
        loads.append(
            pltpu.make_async_copy(
                traces_ref.at[s], tr.at[pl.ds(s * per_shot, per_shot)], load_sem.at[s]
            )
        )
        loads[-1].start()
    wloads = []
    for s in range(shots):
        wloads.append(
            pltpu.make_async_copy(
                weights_ref.at[s, pl.ds(2 * z, 2)], wt.at[pl.ds(2 * s, 2)], wload_sem.at[s]
            )
        )
        wloads[-1].start()

    sub = lax.broadcasted_iota(jnp.int32, (ROWS, 128), 0)
    ids = jnp.zeros((ROWS, 128), jnp.int32)
    for r in range(ROWS):
        ids = jnp.where(sub == r, ids_ref[r // 2, 2 * z + r % 2], ids)
    id_send[...] = ids
    id_recv[0] = ids
    fsend[...] = jnp.zeros_like(fsend)

    for s in range(shots):
        loads[s].wait()
        for h in range(2):
            rows = pl.ds(s * per_shot + h * 128, 128)
            tr_hi[rows, :], tr_lo[rows, :] = split(tr[rows, :])
    for s in range(shots):
        wloads[s].wait()
    for r in range(ROWS):
        wt_hi[r], wt_lo[r] = split(wt[r])

    def make(s):
        odd = s % 2
        off = odd * ((7 - s) // 2) + (1 - odd) * (ZS - (8 - s) // 2)
        f = (z + off) % ZS
        turn = turn_ref[f]
        for q in range(4):
            cols = pl.ds(q * 256, 256)
            tc, ts = turn[0:1, q * 256 : q * 256 + 256], turn[1:2, q * 256 : q * 256 + 256]
            c0, s0 = base_ref[0:per, cols], base_ref[per:both, cols]
            hi, lo = split(c0 * tc - s0 * ts)
            table[0:per, cols] = hi
            table[both : both + per, cols] = lo
            hi, lo = split(-(s0 * tc + c0 * ts))
            table[per:both, cols] = hi
            table[both + per : 2 * both, cols] = lo
        for pair in range(4):
            rows = pl.ds(pair * 256, 256)
            big = nt_dot(table[...], tr_hi[rows, :])
            spec = big[0:both] + big[both:] + nt_dot(table[0:both, :], tr_lo[rows, :])
            for h in range(2):
                r = pair * 2 + h
                hi, lo = split(spec[:, h * 128 : h * 128 + 128])
                two = nn_dot(jnp.concatenate([hi, lo], axis=0), wt_hi[r])
                part = two[0:both] + two[both:] + nn_dot(hi, wt_lo[r])
                send[s, pl.ds(r, both, stride=ROWS), :] = part

    def block(p):
        return pl.ds(pl.multiple_of(p * share * ROWS, share * ROWS), share * ROWS)

    def post(s):
        pltpu.make_async_copy(send.at[s, block(me)], recv.at[s, 0], self_sem.at[s]).start()

        def one(r, carry):
            p = peer(r)
            pltpu.make_async_remote_copy(
                src_ref=send.at[s, block(p)],
                dst_ref=recv.at[s, r],
                send_sem=send_sem.at[s],
                recv_sem=recv_sem.at[s],
                device_id=(p, z),
                device_id_type=MESH,
            ).start()
            return carry

        lax.fori_loop(1, PLANE, one, 0)

    def take(s):
        pltpu.make_async_copy(send.at[s, block(me)], recv.at[s, 0], self_sem.at[s]).wait()
        got = recv.at[s, pl.ds(1, PLANE - 1)]
        pltpu.make_async_copy(got, got, recv_sem.at[s]).wait()
        for i in range(share):
            data = recv[s, :, i * ROWS : i * ROWS + ROWS, :].reshape(PLANE * ROWS, 128)
            hi, lo = split(data)
            sums = nn_dot(onehot[...], jnp.concatenate([hi, lo], axis=1))
            zsend[s, i * tiles : (i + 1) * tiles, :] = sums[:, 0:128] + sums[:, 128:256]

        @pl.when(s >= 2)
        def _():
            came = zrecv.at[s]
            pltpu.make_async_copy(came, came, zrecv_sem.at[s]).wait()
            zsend[s] = zsend[s] + zrecv[s]

        @pl.when(s < ZS - 1)
        def _():
            pltpu.make_async_remote_copy(
                src_ref=zsend.at[s],
                dst_ref=zrecv.at[s + 2],
                send_sem=zsend_sem.at[s],
                recv_sem=zrecv_sem.at[s + 2],
                device_id=(me, (z + ZS + 2 * (s % 2) - 1) % ZS),
                device_id_type=MESH,
            ).start()

    make(0)
    pl.semaphore_wait(barrier, PLANE - 1 + 2)

    def tell(r, carry):
        pltpu.make_async_remote_copy(
            src_ref=id_send,
            dst_ref=id_recv.at[r],
            send_sem=id_send_sem,
            recv_sem=id_recv_sem,
            device_id=(peer(r), z),
            device_id_type=MESH,
        ).start()
        return carry

    lax.fori_loop(1, PLANE, tell, 0)
    post(0)
    got_ids = id_recv.at[pl.ds(1, PLANE - 1)]

    def body(u, carry):
        @pl.when(u < ZS)
        def _():
            make(u)
            post(u)

        @pl.when(u == 1)
        def _():
            pltpu.make_async_copy(got_ids, got_ids, id_recv_sem).wait()
            lane = lax.broadcasted_iota(jnp.int32, (PLANE * ROWS, 128), 1)
            tile = jnp.where(lane < tiles, lane % PLANE * TILES_DEV + lane // PLANE, -1)
            hit = id_recv[...].reshape(PLANE * ROWS, 128) == tile
            turned = jnp.where(hit, 1.0, 0.0).astype(jnp.float32).T
            onehot[...] = turned[0:tiles].astype(jnp.bfloat16)

        @pl.when(u >= 2)
        def _():
            take(u - 2)

        return carry

    lax.fori_loop(1, ZS + 2, body, 0)

    last = zrecv.at[ZS]
    pltpu.make_async_copy(last, last, zrecv_sem.at[ZS]).wait()
    for i in range(share):
        rows = slice(i * tiles, (i + 1) * tiles)
        total = zsend[ZS - 1, rows, :] + zrecv[ZS, rows, :]
        for t in range(TILES_DEV):
            fsend[pl.ds(i * TILES_DEV + t, PLANE, stride=8), :] = total[
                t * PLANE : (t + 1) * PLANE
            ]

    def eight(p):
        return pl.ds(pl.multiple_of(p * 8, 8), 8)

    own = pltpu.make_async_copy(fsend.at[eight(me)], frecv.at[eight(me)], fself_sem)
    own.start()

    def finish(r, carry):
        p = peer(r)
        pltpu.make_async_remote_copy(
            src_ref=fsend.at[eight(p)],
            dst_ref=frecv.at[eight(me)],
            send_sem=fsend_sem,
            recv_sem=frecv_sem,
            device_id=(p, z),
            device_id_type=MESH,
        ).start()
        return carry

    lax.fori_loop(1, PLANE, finish, 0)
    own.wait()
    most = frecv.at[pl.ds(0, (PLANE - 1) * 8)]
    pltpu.make_async_copy(most, most, frecv_sem).wait()
    for t in range(TILES_DEV):
        for i in range(share):
            out_ref[t, pl.ds(i, PLANE, stride=share), :] = frecv[
                pl.ds(i * TILES_DEV + t, PLANE, stride=8), :
            ]

    pltpu.make_async_copy(most, most, fsend_sem).wait()
    pltpu.make_async_copy(got_ids, got_ids, id_send_sem).wait()

    def drain(s, carry):
        gone = send.at[s, pl.ds(0, (PLANE - 1) * share * ROWS)]
        pltpu.make_async_copy(gone, gone, send_sem.at[s]).wait()

        @pl.when(s < ZS - 1)
        def _():
            left = zsend.at[s]
            pltpu.make_async_copy(left, left, zsend_sem.at[s]).wait()

        return carry

    lax.fori_loop(0, ZS, drain, 0)


def shards(traces, interp_weights, tile_ids):
    shots, recs, time_len = traces.shape
    per = NF // ZS
    both = 2 * per
    share = both // PLANE
    tiles = PLANE * TILES_DEV
    block_len, tile_len = interp_weights.shape[2:]
    base, turn = tables(time_len, per)
    total = shots * recs
    vmem = pl.BlockSpec(memory_space=pltpu.VMEM)
    anywhere = pl.BlockSpec(memory_space=pl.ANY)
    dma = pltpu.SemaphoreType.DMA
    f32, bf16 = jnp.float32, jnp.bfloat16
    binned = pl.pallas_call(
        kernel,
        out_shape=jax.ShapeDtypeStruct((TILES_DEV, both, tile_len), f32),
        in_specs=[pl.BlockSpec(memory_space=pltpu.SMEM), vmem, vmem, anywhere, anywhere],
        out_specs=vmem,
        scratch_shapes=[
            pltpu.VMEM((total, time_len), f32),
            pltpu.VMEM((total, time_len), bf16),
            pltpu.VMEM((total, time_len), bf16),
            pltpu.VMEM((ROWS, block_len, tile_len), f32),
            pltpu.VMEM((ROWS, block_len, tile_len), bf16),
            pltpu.VMEM((ROWS, block_len, tile_len), bf16),
            pltpu.VMEM((2 * both, time_len), bf16),
            pltpu.VMEM((ZS, both * ROWS, tile_len), f32),
            pltpu.VMEM((ZS, PLANE, share * ROWS, tile_len), f32),
            pltpu.VMEM((ZS, share * tiles, tile_len), f32),
            pltpu.VMEM((ZS + 1, share * tiles, tile_len), f32),
            pltpu.VMEM((ROWS, 128), jnp.int32),
            pltpu.VMEM((PLANE, ROWS, 128), jnp.int32),
            pltpu.VMEM((tiles, PLANE * ROWS), bf16),
            pltpu.VMEM((PLANE * 8, tile_len), f32),
            pltpu.VMEM((PLANE * 8, tile_len), f32),
            dma((shots,)), dma((shots,)), dma((ZS,)), dma((ZS,)), dma((ZS,)),
            dma((ZS,)), dma((ZS + 1,)), dma, dma, dma, dma, dma,
        ],
        compiler_params=pltpu.CompilerParams(collective_id=0, has_side_effects=True),
    )(tile_ids, jnp.asarray(base), jnp.asarray(turn), traces, interp_weights)
    return binned.reshape(TILES_DEV, 2, per, tile_len)


def solution(mesh):
    in_specs = (P("shot", "freq", None), P("shot", None, None, None), P("shot", None))
    out_specs = P("shot", None, "freq", None)
    return jax.shard_map(shards, mesh=mesh, in_specs=in_specs, out_specs=out_specs, check_vma=False)
```

```python
import math

import jax
import jax.numpy as jnp
import numpy as np
from jax import lax
from jax.experimental import pallas as pl
from jax.experimental.pallas import tpu as pltpu
from jax.sharding import PartitionSpec as P

NF = 384
TILES_DEV = 2
YS, XS, CS = 4, 4, 2
PLANE = YS * XS * CS
ZS = 8
ROWS = 8
WIDE = 2
SIDE = 2
SLOT = 16
MESH = pl.DeviceIdType.MESH


def tables(time_len, per):
    t = np.arange(time_len)
    low = 2.0 * math.pi / time_len * (np.arange(per)[:, None] * t[None, :] % time_len)
    base = np.concatenate([np.cos(low), np.sin(low)]) / math.sqrt(time_len)
    high = 2.0 * math.pi / time_len * ((np.arange(ZS) * per)[:, None] * t[None, :] % time_len)
    turn = np.stack([np.cos(high), np.sin(high)], axis=1)
    return base.astype(np.float32), turn.astype(np.float32)


def split(value):
    high = value.astype(jnp.bfloat16)
    return high, (value - high.astype(jnp.float32)).astype(jnp.bfloat16)


def nt_dot(a, b):
    return lax.dot_general(a, b, (((1,), (1,)), ((), ())), preferred_element_type=jnp.float32)


def nn_dot(a, b):
    return jnp.dot(a, b, preferred_element_type=jnp.float32)


def kernel(
    ids_ref, base_hbm, turn_hbm, traces_ref, weights_ref, out_ref,
    base_ref, turn_ref, tr, tr_hi, tr_lo, wt, wt_hi, wt_lo, table, send, recv, xrecv, yrecv,
    zsend, zrecv, id_send, id_recv, onehot, yhot, fsend, frecv,
    table_sem, load_sem, wload_sem, send_sem, recv_sem, self_sem, xsend_sem, xrecv_sem, xself_sem,
    ysend_sem, yrecv_sem, yself_sem, zsend_sem, zrecv_sem,
    id_send_sem, id_recv_sem, fsend_sem, frecv_sem, fself_sem,
):
    per = base_ref.shape[0] // 2
    both = 2 * per
    parts = WIDE + 2 * SIDE
    xfrom = PLANE * WIDE
    yfrom = xfrom + XS * CS * SIDE
    tiles = PLANE * TILES_DEV
    me = lax.axis_index("shot")
    z = lax.axis_index("freq")
    core = me % CS
    x = me // CS % XS
    y = me // (CS * XS)

    rows_at = [(y + d) % YS * (XS * CS) for d in range(YS)]
    cols_at = [(x + d) % XS * CS for d in range(XS)]
    cores_at = [core, (core + 1) % CS]

    def peer(r):
        return rows_at[r // (CS * XS)] + cols_at[r // CS % XS] + cores_at[r % CS]

    far_first = sorted(
        range(1, PLANE),
        key=lambda r: -min(r // 8, 4 - r // 8) - min(r // 2 % 4, 4 - r // 2 % 4),
    )

    barrier = pltpu.get_barrier_semaphore()

    def greet(r):
        pl.semaphore_signal(barrier, inc=1, device_id=(peer(r), z), device_id_type=MESH)

    for r in far_first:
        greet(r)
    for step in (1, ZS - 1):
        pl.semaphore_signal(
            barrier, inc=1, device_id=(me, (z + step) % ZS), device_id_type=MESH
        )

    shots = traces_ref.shape[0]
    per_shot = traces_ref.shape[1]
    first = [
        pltpu.make_async_copy(base_hbm, base_ref, table_sem.at[0]),
        pltpu.make_async_copy(turn_hbm, turn_ref, table_sem.at[1]),
    ]
    for copy in first:
        copy.start()
    wloads = []
    for s in range(shots):
        wloads.append(
            pltpu.make_async_copy(
                weights_ref.at[s, pl.ds(2 * z, 2)], wt.at[pl.ds(2 * s, 2)], wload_sem.at[s]
            )
        )
        wloads[-1].start()

    loads = []
    for s in range(shots):
        loads.append(
            pltpu.make_async_copy(
                traces_ref.at[s], tr.at[pl.ds(s * per_shot, per_shot)], load_sem.at[s]
            )
        )
        loads[-1].start()
    lane = lax.broadcasted_iota(jnp.int32, (1, 128), 1)
    ids = jnp.zeros((1, 128), jnp.int32)
    for r in range(ROWS):
        ids = jnp.where(lane % ROWS == r, ids_ref[r // 2, 2 * z + r % 2], ids)
    id_send[...] = ids
    id_recv[0] = ids
    fsend[...] = jnp.zeros_like(fsend)

    def tabulate(s):
        odd = s % 2
        off = odd * ((7 - s) // 2) + (1 - odd) * (ZS - (8 - s) // 2)
        f = (z + off) % ZS
        turn = turn_ref[f]
        for q in range(4):
            cols = pl.ds(q * 256, 256)
            tc, ts = turn[0:1, q * 256 : q * 256 + 256], turn[1:2, q * 256 : q * 256 + 256]
            c0, s0 = base_ref[0:per, cols], base_ref[per:both, cols]
            hi, lo = split(c0 * tc - s0 * ts)
            table[0:per, cols] = hi
            table[both : both + per, cols] = lo
            hi, lo = split(-(s0 * tc + c0 * ts))
            table[per:both, cols] = hi
            table[both + per : 2 * both, cols] = lo

    def project(s, pair):
        rows = pl.ds(pair * 256, 256)
        big = nt_dot(table[...], tr_hi[rows, :])
        spec = big[0:both] + big[both:] + nt_dot(table[0:both, :], tr_lo[rows, :])
        for h in range(2):
            r = pair * 2 + h
            hi, lo = split(spec[:, h * 128 : h * 128 + 128])
            two = nn_dot(jnp.concatenate([hi, lo], axis=0), wt_hi[r])
            part = two[0:both] + two[both:] + nn_dot(hi, wt_lo[r])
            send[s, pl.ds(r, both, stride=ROWS), :] = part

    def make(s):
        tabulate(s)
        for pair in range(shots):
            project(s, pair)

    def make_first():
        for copy in first:
            copy.wait()
        tabulate(0)
        for s in range(shots):
            wloads[s].wait()
        for r in range(ROWS):
            wt_hi[r], wt_lo[r] = split(wt[r])
        for s in range(shots):
            loads[s].wait()
            for h in range(2):
                rows = pl.ds(s * per_shot + h * 128, 128)
                tr_hi[rows, :], tr_lo[rows, :] = split(tr[rows, :])
            project(0, s)

    def rows_of(first_row, index, count):
        start = pl.multiple_of((first_row + index * count) * ROWS, ROWS)
        return pl.ds(start, count * ROWS)

    def xpeer(j):
        index = cols_at[j // CS] + cores_at[j % CS]
        return index, rows_at[0] + index

    def ypeer(j):
        place, pc = rows_at[j // CS], cores_at[j % CS]
        return place // XS + pc, place + cols_at[0] + pc

    def own_copies(s):
        return [
            pltpu.make_async_copy(
                send.at[s, rows_of(0, me, WIDE)], recv.at[s, 0], self_sem.at[s]
            ),
            pltpu.make_async_copy(
                send.at[s, rows_of(xfrom, xpeer(0)[0], SIDE)], xrecv.at[s, 0], xself_sem.at[s]
            ),
            pltpu.make_async_copy(
                send.at[s, rows_of(yfrom, ypeer(0)[0], SIDE)], yrecv.at[s, 0], yself_sem.at[s]
            ),
        ]

    def post(s):
        for copy in own_copies(s):
            copy.start()

        def side(j):
            index, p = xpeer(j)
            pltpu.make_async_remote_copy(
                src_ref=send.at[s, rows_of(xfrom, index, SIDE)],
                dst_ref=xrecv.at[s, j],
                send_sem=xsend_sem.at[s],
                recv_sem=xrecv_sem.at[s],
                device_id=(p, z),
                device_id_type=MESH,
            ).start()
            index, p = ypeer(j)
            pltpu.make_async_remote_copy(
                src_ref=send.at[s, rows_of(yfrom, index, SIDE)],
                dst_ref=yrecv.at[s, j],
                send_sem=ysend_sem.at[s],
                recv_sem=yrecv_sem.at[s],
                device_id=(p, z),
                device_id_type=MESH,
            ).start()

        def one(r):
            p = peer(r)
            pltpu.make_async_remote_copy(
                src_ref=send.at[s, rows_of(0, p, WIDE)],
                dst_ref=recv.at[s, r],
                send_sem=send_sem.at[s],
                recv_sem=recv_sem.at[s],
                device_id=(p, z),
                device_id_type=MESH,
            ).start()

        for r in range(1, PLANE):
            one(r)
        for r in range(1, XS * CS):
            side(r)

    def gather(hot, data, s, part):
        hi, lo = split(data)
        sums = nn_dot(hot, jnp.concatenate([hi, lo], axis=1))
        zsend[s, part * tiles : (part + 1) * tiles, :] = sums[:, 0:128] + sums[:, 128:256]

    def take(s):
        for copy in own_copies(s):
            copy.wait()
        for ref, sem in ((xrecv, xrecv_sem), (yrecv, yrecv_sem), (recv, recv_sem)):
            got = ref.at[s, pl.ds(1, ref.shape[1] - 1)]
            pltpu.make_async_copy(got, got, sem.at[s]).wait()
        near = XS * CS * ROWS
        for i in range(SIDE):
            rows = slice(i * ROWS, i * ROWS + ROWS)
            gather(onehot[:, 0:near], xrecv[s, :, rows, :].reshape(near, 128), s, WIDE + i)
            gather(yhot[...], yrecv[s, :, rows, :].reshape(near, 128), s, WIDE + SIDE + i)
        for i in range(WIDE):
            data = recv[s, :, i * ROWS : i * ROWS + ROWS, :].reshape(PLANE * ROWS, 128)
            gather(onehot[...], data, s, i)

        @pl.when(s >= 2)
        def _():
            came = zrecv.at[s]
            pltpu.make_async_copy(came, came, zrecv_sem.at[s]).wait()
            zsend[s] = zsend[s] + zrecv[s]

        @pl.when(s < ZS - 1)
        def _():
            pltpu.make_async_remote_copy(
                src_ref=zsend.at[s],
                dst_ref=zrecv.at[s + 2],
                send_sem=zsend_sem.at[s],
                recv_sem=zrecv_sem.at[s + 2],
                device_id=(me, (z + ZS + 2 * (s % 2) - 1) % ZS),
                device_id_type=MESH,
            ).start()

    make_first()
    pl.semaphore_wait(barrier, PLANE - 1 + 2)

    def tell(r):
        pltpu.make_async_remote_copy(
            src_ref=id_send,
            dst_ref=id_recv.at[r],
            send_sem=id_send_sem,
            recv_sem=id_recv_sem,
            device_id=(peer(r), z),
            device_id_type=MESH,
        ).start()

    post(0)
    for r in far_first:
        tell(r)
    make(1)
    got_ids = id_recv.at[pl.ds(1, PLANE - 1)]

    def body(u, carry):
        @pl.when(u < ZS)
        def _():
            post(u)

        @pl.when(u < ZS - 1)
        def _():
            make(u + 1)

        @pl.when(u == 1)
        def _():
            pltpu.make_async_copy(got_ids, got_ids, id_recv_sem).wait()
            rho = lax.broadcasted_iota(jnp.int32, (tiles, 128), 0)
            tile = rho % PLANE * TILES_DEV + rho // PLANE
            for half in range(2):
                row = jnp.zeros((1, 128), jnp.int32)
                for slot in range(16):
                    row = jnp.where(lane // ROWS == slot, id_recv[half * 16 + slot], row)
                hit = jnp.where(tile == row, 1.0, 0.0).astype(jnp.float32)
                onehot[:, half * 128 : half * 128 + 128] = hit.astype(jnp.bfloat16)
            row = jnp.zeros((1, 128), jnp.int32)
            for j in range(YS * CS):
                row = jnp.where(lane // ROWS == j, id_recv[j // CS * XS * CS + j % CS], row)
            hit = jnp.where(tile == row, 1.0, 0.0).astype(jnp.float32)
            yhot[...] = hit[:, 0 : YS * CS * ROWS].astype(jnp.bfloat16)

        @pl.when(u >= 1)
        def _():
            take(u - 1)

        return carry

    lax.fori_loop(1, ZS + 1, body, 0)

    last = zrecv.at[ZS]
    pltpu.make_async_copy(last, last, zrecv_sem.at[ZS]).wait()
    for i in range(parts):
        rows = slice(i * tiles, (i + 1) * tiles)
        total = zsend[ZS - 1, rows, :] + zrecv[ZS, rows, :]
        for t in range(TILES_DEV):
            fsend[pl.ds(i * TILES_DEV + t, PLANE, stride=SLOT), :] = total[
                t * PLANE : (t + 1) * PLANE
            ]

    def slot(p):
        return pl.ds(pl.multiple_of(p * SLOT, SLOT), SLOT)

    own = pltpu.make_async_copy(fsend.at[slot(me)], frecv.at[slot(me)], fself_sem)
    own.start()

    def finish(r):
        p = peer(r)
        pltpu.make_async_remote_copy(
            src_ref=fsend.at[slot(p)],
            dst_ref=frecv.at[slot(me)],
            send_sem=fsend_sem,
            recv_sem=frecv_sem,
            device_id=(p, z),
            device_id_type=MESH,
        ).start()

    for r in far_first:
        finish(r)
    own.wait()
    most = frecv.at[pl.ds(0, (PLANE - 1) * SLOT)]
    pltpu.make_async_copy(most, most, frecv_sem).wait()
    for t in range(TILES_DEV):
        for i in range(WIDE):
            out_ref[t, pl.ds(i, PLANE, stride=WIDE), :] = frecv[
                pl.ds(i * TILES_DEV + t, PLANE, stride=SLOT), :
            ]
        for i in range(SIDE):
            row = (WIDE + i) * TILES_DEV + t
            count = XS * CS
            total = frecv[pl.ds(row, count, stride=SLOT), :]
            for py in range(1, YS):
                total = total + frecv[pl.ds(py * count * SLOT + row, count, stride=SLOT), :]
            out_ref[t, pl.ds(xfrom + i, count, stride=SIDE), :] = total
            row = (WIDE + SIDE + i) * TILES_DEV + t
            for pc in range(CS):
                total = frecv[pl.ds(pc * SLOT + row, YS, stride=count * SLOT), :]
                for px in range(1, XS):
                    start = (px * CS + pc) * SLOT + row
                    total = total + frecv[pl.ds(start, YS, stride=count * SLOT), :]
                out_ref[t, pl.ds(yfrom + pc * SIDE + i, YS, stride=CS * SIDE), :] = total

    pltpu.make_async_copy(most, most, fsend_sem).wait()
    pltpu.make_async_copy(got_ids, got_ids, id_send_sem).wait()

    def drain(s, carry):
        for ref, sem in ((xrecv, xsend_sem), (yrecv, ysend_sem), (recv, send_sem)):
            gone = ref.at[s, pl.ds(1, ref.shape[1] - 1)]
            pltpu.make_async_copy(gone, gone, sem.at[s]).wait()

        @pl.when(s < ZS - 1)
        def _():
            left = zsend.at[s]
            pltpu.make_async_copy(left, left, zsend_sem.at[s]).wait()

        return carry

    lax.fori_loop(0, ZS, drain, 0)


def shards(traces, interp_weights, tile_ids):
    shots, recs, time_len = traces.shape
    per = NF // ZS
    both = 2 * per
    parts = WIDE + 2 * SIDE
    tiles = PLANE * TILES_DEV
    block_len, tile_len = interp_weights.shape[2:]
    base, turn = tables(time_len, per)
    total = shots * recs
    vmem = pl.BlockSpec(memory_space=pltpu.VMEM)
    hbm = pl.BlockSpec(memory_space=pltpu.HBM)
    dma = pltpu.SemaphoreType.DMA
    f32, bf16 = jnp.float32, jnp.bfloat16
    binned = pl.pallas_call(
        kernel,
        out_shape=jax.ShapeDtypeStruct((TILES_DEV, both, tile_len), f32),
        in_specs=[pl.BlockSpec(memory_space=pltpu.SMEM)] + [hbm] * 4,
        out_specs=vmem,
        scratch_shapes=[
            pltpu.VMEM(base.shape, f32),
            pltpu.VMEM(turn.shape, f32),
            pltpu.VMEM((total, time_len), f32),
            pltpu.VMEM((total, time_len), bf16),
            pltpu.VMEM((total, time_len), bf16),
            pltpu.VMEM((ROWS, block_len, tile_len), f32),
            pltpu.VMEM((ROWS, block_len, tile_len), bf16),
            pltpu.VMEM((ROWS, block_len, tile_len), bf16),
            pltpu.VMEM((2 * both, time_len), bf16),
            pltpu.VMEM((ZS, both * ROWS, tile_len), f32),
            pltpu.VMEM((ZS, PLANE, WIDE * ROWS, tile_len), f32),
            pltpu.VMEM((ZS, XS * CS, SIDE * ROWS, tile_len), f32),
            pltpu.VMEM((ZS, YS * CS, SIDE * ROWS, tile_len), f32),
            pltpu.VMEM((ZS, parts * tiles, tile_len), f32),
            pltpu.VMEM((ZS + 1, parts * tiles, tile_len), f32),
            pltpu.VMEM((1, 128), jnp.int32),
            pltpu.VMEM((PLANE, 1, 128), jnp.int32),
            pltpu.VMEM((tiles, PLANE * ROWS), bf16),
            pltpu.VMEM((tiles, YS * CS * ROWS), bf16),
            pltpu.VMEM((PLANE * SLOT, tile_len), f32),
            pltpu.VMEM((PLANE * SLOT, tile_len), f32),
            dma((2,)), dma((shots,)), dma((shots,)), dma((ZS,)), dma((ZS,)), dma((ZS,)),
            dma((ZS,)), dma((ZS,)), dma((ZS,)), dma((ZS,)), dma((ZS,)), dma((ZS,)),
            dma((ZS,)), dma((ZS + 1,)), dma, dma, dma, dma, dma,
        ],
        compiler_params=pltpu.CompilerParams(collective_id=0, has_side_effects=True),
    )(tile_ids, jnp.asarray(base), jnp.asarray(turn), traces, interp_weights)
    return binned.reshape(TILES_DEV, 2, per, tile_len)


def solution(mesh):
    in_specs = (P("shot", "freq", None), P("shot", None, None, None), P("shot", None))
    out_specs = P("shot", None, "freq", None)
    return jax.shard_map(shards, mesh=mesh, in_specs=in_specs, out_specs=out_specs, check_vma=False)
```

```python
import math

import jax
import jax.numpy as jnp
import numpy as np
from jax import lax
from jax.experimental import pallas as pl
from jax.experimental.pallas import tpu as pltpu
from jax.sharding import PartitionSpec as P

NF = 384
TILES_DEV = 2
YS, XS, CS = 4, 4, 2
PLANE = YS * XS * CS
ZS = 8
ROWS = 8
WIDE = 2
SIDE = 2
SLOT = 16
MESH = pl.DeviceIdType.MESH


def tables(time_len, per):
    t = np.arange(time_len)
    low = 2.0 * math.pi / time_len * (np.arange(per)[:, None] * t[None, :] % time_len)
    base = np.concatenate([np.cos(low), np.sin(low)]) / math.sqrt(time_len)
    high = 2.0 * math.pi / time_len * ((np.arange(ZS) * per)[:, None] * t[None, :] % time_len)
    turn = np.stack([np.cos(high), np.sin(high)], axis=1)
    return base.astype(np.float32), turn.astype(np.float32)


def split(value):
    high = value.astype(jnp.bfloat16)
    return high, (value - high.astype(jnp.float32)).astype(jnp.bfloat16)


def nt_dot(a, b):
    return lax.dot_general(a, b, (((1,), (1,)), ((), ())), preferred_element_type=jnp.float32)


def nn_dot(a, b):
    return jnp.dot(a, b, preferred_element_type=jnp.float32)


def kernel(
    ids_ref, base_hbm, turn_hbm, traces_ref, weights_ref, out_ref,
    base_ref, turn_ref, tr, tr_hi, tr_lo, wt, wt_hi, wt_lo, table, send, recv, xrecv, yrecv,
    zsend, zrecv, id_send, id_recv, onehot, yhot, fsend, frecv,
    table_sem, load_sem, wload_sem, send_sem, recv_sem, self_sem, xsend_sem, xrecv_sem, xself_sem,
    ysend_sem, yrecv_sem, yself_sem, zsend_sem, zrecv_sem,
    id_send_sem, id_recv_sem, fsend_sem, frecv_sem, fself_sem,
):
    per = base_ref.shape[0] // 2
    both = 2 * per
    parts = WIDE + 2 * SIDE
    xfrom = PLANE * WIDE
    yfrom = xfrom + XS * CS * SIDE
    tiles = PLANE * TILES_DEV
    me = lax.axis_index("shot")
    z = lax.axis_index("freq")
    core = me % CS
    x = me // CS % XS
    y = me // (CS * XS)

    rows_at = [(y + d) % YS * (XS * CS) for d in range(YS)]
    cols_at = [(x + d) % XS * CS for d in range(XS)]
    cores_at = [core, (core + 1) % CS]

    def peer(r):
        return rows_at[r // (CS * XS)] + cols_at[r // CS % XS] + cores_at[r % CS]

    far_first = sorted(
        range(1, PLANE),
        key=lambda r: -min(r // 8, 4 - r // 8) - min(r // 2 % 4, 4 - r // 2 % 4),
    )

    barrier = pltpu.get_barrier_semaphore()

    def greet(r):
        pl.semaphore_signal(barrier, inc=1, device_id=(peer(r), z), device_id_type=MESH)

    for r in far_first:
        greet(r)
    for step in (1, ZS - 1):
        pl.semaphore_signal(
            barrier, inc=1, device_id=(me, (z + step) % ZS), device_id_type=MESH
        )

    shots = traces_ref.shape[0]
    per_shot = traces_ref.shape[1]
    first = [
        pltpu.make_async_copy(base_hbm, base_ref, table_sem.at[0]),
        pltpu.make_async_copy(turn_hbm, turn_ref, table_sem.at[1]),
    ]
    for copy in first:
        copy.start()
    wloads = []
    for s in range(shots):
        wloads.append(
            pltpu.make_async_copy(
                weights_ref.at[s, pl.ds(2 * z, 2)], wt.at[pl.ds(2 * s, 2)], wload_sem.at[s]
            )
        )
        wloads[-1].start()

    loads = []
    for s in range(shots):
        loads.append(
            pltpu.make_async_copy(
                traces_ref.at[s], tr.at[pl.ds(s * per_shot, per_shot)], load_sem.at[s]
            )
        )
        loads[-1].start()
    lane = lax.broadcasted_iota(jnp.int32, (1, 128), 1)
    ids = jnp.zeros((1, 128), jnp.int32)
    for r in range(ROWS):
        ids = jnp.where(lane % ROWS == r, ids_ref[r // 2, 2 * z + r % 2], ids)
    id_send[...] = ids
    id_recv[0] = ids
    fsend[...] = jnp.zeros_like(fsend)

    def tabulate(s):
        odd = s % 2
        off = odd * ((7 - s) // 2) + (1 - odd) * (ZS - (8 - s) // 2)
        f = (z + off) % ZS
        turn = turn_ref[f]
        for q in range(4):
            cols = pl.ds(q * 256, 256)
            tc, ts = turn[0:1, q * 256 : q * 256 + 256], turn[1:2, q * 256 : q * 256 + 256]
            c0, s0 = base_ref[0:per, cols], base_ref[per:both, cols]
            hi, lo = split(c0 * tc - s0 * ts)
            table[0:per, cols] = hi
            table[both : both + per, cols] = lo
            hi, lo = split(-(s0 * tc + c0 * ts))
            table[per:both, cols] = hi
            table[both + per : 2 * both, cols] = lo

    def project(s, pair):
        rows = pl.ds(pair * 256, 256)
        big = nt_dot(table[...], tr_hi[rows, :])
        spec = big[0:both] + big[both:] + nt_dot(table[0:both, :], tr_lo[rows, :])
        for h in range(2):
            r = pair * 2 + h
            hi, lo = split(spec[:, h * 128 : h * 128 + 128])
            two = nn_dot(jnp.concatenate([hi, lo], axis=0), wt_hi[r])
            part = two[0:both] + two[both:] + nn_dot(hi, wt_lo[r])
            send[s, pl.ds(r, both, stride=ROWS), :] = part

    def make(s):
        tabulate(s)
        for pair in range(shots):
            project(s, pair)

    def make_first():
        for copy in first:
            copy.wait()
        tabulate(0)
        for s in range(shots):
            wloads[s].wait()
        for r in range(ROWS):
            wt_hi[r], wt_lo[r] = split(wt[r])
        for s in range(shots):
            loads[s].wait()
            for h in range(2):
                rows = pl.ds(s * per_shot + h * 128, 128)
                tr_hi[rows, :], tr_lo[rows, :] = split(tr[rows, :])
            project(0, s)

    def rows_of(first_row, index, count):
        start = pl.multiple_of((first_row + index * count) * ROWS, ROWS)
        return pl.ds(start, count * ROWS)

    def xpeer(j):
        index = cols_at[j // CS] + cores_at[j % CS]
        return index, rows_at[0] + index

    def ypeer(j):
        place, pc = rows_at[j // CS], cores_at[j % CS]
        return place // XS + pc, place + cols_at[0] + pc

    def own_copies(s):
        return [
            pltpu.make_async_copy(
                send.at[s, rows_of(0, me, WIDE)], recv.at[s, 0], self_sem.at[s]
            ),
            pltpu.make_async_copy(
                send.at[s, rows_of(xfrom, xpeer(0)[0], SIDE)], xrecv.at[s, 0], xself_sem.at[s]
            ),
            pltpu.make_async_copy(
                send.at[s, rows_of(yfrom, ypeer(0)[0], SIDE)], yrecv.at[s, 0], yself_sem.at[s]
            ),
        ]

    def post(s):
        for copy in own_copies(s):
            copy.start()

        def side(j):
            index, p = xpeer(j)
            pltpu.make_async_remote_copy(
                src_ref=send.at[s, rows_of(xfrom, index, SIDE)],
                dst_ref=xrecv.at[s, j],
                send_sem=xsend_sem.at[s],
                recv_sem=xrecv_sem.at[s],
                device_id=(p, z),
                device_id_type=MESH,
            ).start()
            index, p = ypeer(j)
            pltpu.make_async_remote_copy(
                src_ref=send.at[s, rows_of(yfrom, index, SIDE)],
                dst_ref=yrecv.at[s, j],
                send_sem=ysend_sem.at[s],
                recv_sem=yrecv_sem.at[s],
                device_id=(p, z),
                device_id_type=MESH,
            ).start()

        def one(r):
            p = peer(r)
            pltpu.make_async_remote_copy(
                src_ref=send.at[s, rows_of(0, p, WIDE)],
                dst_ref=recv.at[s, r],
                send_sem=send_sem.at[s],
                recv_sem=recv_sem.at[s],
                device_id=(p, z),
                device_id_type=MESH,
            ).start()

        for r in range(1, PLANE):
            one(r)
        for r in range(1, XS * CS):
            side(r)

    def gather(hot, data, s, part):
        hi, lo = split(data)
        sums = nn_dot(hot, jnp.concatenate([hi, lo], axis=1))
        zsend[s, part * tiles : (part + 1) * tiles, :] = sums[:, 0:128] + sums[:, 128:256]

    def take(s):
        for copy in own_copies(s):
            copy.wait()
        for ref, sem in ((xrecv, xrecv_sem), (yrecv, yrecv_sem), (recv, recv_sem)):
            got = ref.at[s, pl.ds(1, ref.shape[1] - 1)]
            pltpu.make_async_copy(got, got, sem.at[s]).wait()
        near = XS * CS * ROWS
        for i in range(SIDE):
            rows = slice(i * ROWS, i * ROWS + ROWS)
            gather(onehot[:, 0:near], xrecv[s, :, rows, :].reshape(near, 128), s, WIDE + i)
            gather(yhot[...], yrecv[s, :, rows, :].reshape(near, 128), s, WIDE + SIDE + i)
        for i in range(WIDE):
            data = recv[s, :, i * ROWS : i * ROWS + ROWS, :].reshape(PLANE * ROWS, 128)
            gather(onehot[...], data, s, i)

        @pl.when(s >= 2)
        def _():
            came = zrecv.at[s]
            pltpu.make_async_copy(came, came, zrecv_sem.at[s]).wait()
            zsend[s] = zsend[s] + zrecv[s]

        @pl.when(s < ZS - 1)
        def _():
            pltpu.make_async_remote_copy(
                src_ref=zsend.at[s],
                dst_ref=zrecv.at[s + 2],
                send_sem=zsend_sem.at[s],
                recv_sem=zrecv_sem.at[s + 2],
                device_id=(me, (z + ZS + 2 * (s % 2) - 1) % ZS),
                device_id_type=MESH,
            ).start()

    make_first()
    pl.semaphore_wait(barrier, PLANE - 1 + 2)

    def tell(r):
        pltpu.make_async_remote_copy(
            src_ref=id_send,
            dst_ref=id_recv.at[r],
            send_sem=id_send_sem,
            recv_sem=id_recv_sem,
            device_id=(peer(r), z),
            device_id_type=MESH,
        ).start()

    post(0)
    make(1)
    for r in far_first:
        tell(r)
    got_ids = id_recv.at[pl.ds(1, PLANE - 1)]

    def body(u, carry):
        @pl.when(u < ZS)
        def _():
            post(u)

        @pl.when(u < ZS - 1)
        def _():
            make(u + 1)

        @pl.when(u == 1)
        def _():
            pltpu.make_async_copy(got_ids, got_ids, id_recv_sem).wait()
            rho = lax.broadcasted_iota(jnp.int32, (tiles, 128), 0)
            tile = rho % PLANE * TILES_DEV + rho // PLANE
            for half in range(2):
                row = jnp.zeros((1, 128), jnp.int32)
                for slot in range(16):
                    row = jnp.where(lane // ROWS == slot, id_recv[half * 16 + slot], row)
                hit = jnp.where(tile == row, 1.0, 0.0).astype(jnp.float32)
                onehot[:, half * 128 : half * 128 + 128] = hit.astype(jnp.bfloat16)
            row = jnp.zeros((1, 128), jnp.int32)
            for j in range(YS * CS):
                row = jnp.where(lane // ROWS == j, id_recv[j // CS * XS * CS + j % CS], row)
            hit = jnp.where(tile == row, 1.0, 0.0).astype(jnp.float32)
            yhot[...] = hit[:, 0 : YS * CS * ROWS].astype(jnp.bfloat16)

        @pl.when(u >= 1)
        def _():
            take(u - 1)

        return carry

    lax.fori_loop(1, ZS + 1, body, 0)

    last = zrecv.at[ZS]
    pltpu.make_async_copy(last, last, zrecv_sem.at[ZS]).wait()
    for i in range(parts):
        rows = slice(i * tiles, (i + 1) * tiles)
        total = zsend[ZS - 1, rows, :] + zrecv[ZS, rows, :]
        for t in range(TILES_DEV):
            fsend[pl.ds(i * TILES_DEV + t, PLANE, stride=SLOT), :] = total[
                t * PLANE : (t + 1) * PLANE
            ]

    def slot(p):
        return pl.ds(pl.multiple_of(p * SLOT, SLOT), parts * TILES_DEV)

    own = pltpu.make_async_copy(fsend.at[slot(me)], frecv.at[slot(me)], fself_sem)
    own.start()

    def finish(r):
        p = peer(r)
        pltpu.make_async_remote_copy(
            src_ref=fsend.at[slot(p)],
            dst_ref=frecv.at[slot(me)],
            send_sem=fsend_sem,
            recv_sem=frecv_sem,
            device_id=(p, z),
            device_id_type=MESH,
        ).start()

    for r in far_first:
        finish(r)
    pltpu.make_async_copy(got_ids, got_ids, id_send_sem).wait()

    def drain(s, carry):
        for ref, sem in ((xrecv, xsend_sem), (yrecv, ysend_sem), (recv, send_sem)):
            gone = ref.at[s, pl.ds(1, ref.shape[1] - 1)]
            pltpu.make_async_copy(gone, gone, sem.at[s]).wait()

        @pl.when(s < ZS - 1)
        def _():
            left = zsend.at[s]
            pltpu.make_async_copy(left, left, zsend_sem.at[s]).wait()

        return carry

    lax.fori_loop(0, ZS, drain, 0)

    own.wait()
    most = frecv.at[pl.ds(0, (PLANE - 1) * parts * TILES_DEV)]
    pltpu.make_async_copy(most, most, frecv_sem).wait()
    for t in range(TILES_DEV):
        for i in range(WIDE):
            out_ref[t, pl.ds(i, PLANE, stride=WIDE), :] = frecv[
                pl.ds(i * TILES_DEV + t, PLANE, stride=SLOT), :
            ]
        for i in range(SIDE):
            row = (WIDE + i) * TILES_DEV + t
            count = XS * CS
            total = frecv[pl.ds(row, count, stride=SLOT), :]
            for py in range(1, YS):
                total = total + frecv[pl.ds(py * count * SLOT + row, count, stride=SLOT), :]
            out_ref[t, pl.ds(xfrom + i, count, stride=SIDE), :] = total
            row = (WIDE + SIDE + i) * TILES_DEV + t
            for pc in range(CS):
                total = frecv[pl.ds(pc * SLOT + row, YS, stride=count * SLOT), :]
                for px in range(1, XS):
                    start = (px * CS + pc) * SLOT + row
                    total = total + frecv[pl.ds(start, YS, stride=count * SLOT), :]
                out_ref[t, pl.ds(yfrom + pc * SIDE + i, YS, stride=CS * SIDE), :] = total

    pltpu.make_async_copy(most, most, fsend_sem).wait()


def shards(traces, interp_weights, tile_ids):
    shots, recs, time_len = traces.shape
    per = NF // ZS
    both = 2 * per
    parts = WIDE + 2 * SIDE
    tiles = PLANE * TILES_DEV
    block_len, tile_len = interp_weights.shape[2:]
    base, turn = tables(time_len, per)
    total = shots * recs
    vmem = pl.BlockSpec(memory_space=pltpu.VMEM)
    hbm = pl.BlockSpec(memory_space=pltpu.HBM)
    dma = pltpu.SemaphoreType.DMA
    f32, bf16 = jnp.float32, jnp.bfloat16
    binned = pl.pallas_call(
        kernel,
        out_shape=jax.ShapeDtypeStruct((TILES_DEV, both, tile_len), f32),
        in_specs=[pl.BlockSpec(memory_space=pltpu.SMEM)] + [hbm] * 4,
        out_specs=vmem,
        scratch_shapes=[
            pltpu.VMEM(base.shape, f32),
            pltpu.VMEM(turn.shape, f32),
            pltpu.VMEM((total, time_len), f32),
            pltpu.VMEM((total, time_len), bf16),
            pltpu.VMEM((total, time_len), bf16),
            pltpu.VMEM((ROWS, block_len, tile_len), f32),
            pltpu.VMEM((ROWS, block_len, tile_len), bf16),
            pltpu.VMEM((ROWS, block_len, tile_len), bf16),
            pltpu.VMEM((2 * both, time_len), bf16),
            pltpu.VMEM((ZS, both * ROWS, tile_len), f32),
            pltpu.VMEM((ZS, PLANE, WIDE * ROWS, tile_len), f32),
            pltpu.VMEM((ZS, XS * CS, SIDE * ROWS, tile_len), f32),
            pltpu.VMEM((ZS, YS * CS, SIDE * ROWS, tile_len), f32),
            pltpu.VMEM((ZS, parts * tiles, tile_len), f32),
            pltpu.VMEM((ZS + 1, parts * tiles, tile_len), f32),
            pltpu.VMEM((1, 128), jnp.int32),
            pltpu.VMEM((PLANE, 1, 128), jnp.int32),
            pltpu.VMEM((tiles, PLANE * ROWS), bf16),
            pltpu.VMEM((tiles, YS * CS * ROWS), bf16),
            pltpu.VMEM((PLANE * SLOT, tile_len), f32),
            pltpu.VMEM((PLANE * SLOT, tile_len), f32),
            dma((2,)), dma((shots,)), dma((shots,)), dma((ZS,)), dma((ZS,)), dma((ZS,)),
            dma((ZS,)), dma((ZS,)), dma((ZS,)), dma((ZS,)), dma((ZS,)), dma((ZS,)),
            dma((ZS,)), dma((ZS + 1,)), dma, dma, dma, dma, dma,
        ],
        compiler_params=pltpu.CompilerParams(collective_id=0, has_side_effects=True),
    )(tile_ids, jnp.asarray(base), jnp.asarray(turn), traces, interp_weights)
    return binned.reshape(TILES_DEV, 2, per, tile_len)


def solution(mesh):
    in_specs = (P("shot", "freq", None), P("shot", None, None, None), P("shot", None))
    out_specs = P("shot", None, "freq", None)
    return jax.shard_map(shards, mesh=mesh, in_specs=in_specs, out_specs=out_specs, check_vma=False)
```
